32 devices in a mesh: feat: 16 (over z, y, x), rows: 2 (over core).
Axes of the slice: x: 2, y: 2, z: 4, core: 2. Of those that a mesh axis runs over, the one named last changes fastest.
Arguments:
- grads: bfloat16 [16384], P(('rows', 'feat')), may hold values from -6 to 6
- hessians: bfloat16 [16384], P(('rows', 'feat')), may hold values from 0.019897461 to 0.25
- nodes: int32 [16384], P(('rows', 'feat')), may hold values from 0 to 15
- bins: int32 [512, 16384], P('feat', 'rows'), may hold values from 0 to 255
Outputs:
- histogram: float32 [2, 16, 512, 256], P(None, 'rows', 'feat')
- best_gain: float32 [16], P('rows')
The draws below stay inside these ranges and needn't reach their ends.
All inputs are finite; a program needn't handle non-finite values.
Results may differ from the reference program's by a relative error of at most 0.0003.
Values may be sent and summed in bfloat16 or wider, within the bound.
A program may use at most 64 MiB of HBM per device.

```python
import math
import jax
import jax.numpy as jnp
from jax import lax

FEAT_DEV = 32
BINS = 256
NODES = 16
FEATURES = 512
ROWS = 16384


def place_ends(entries, own_key, least, top_value):
    shape = entries.shape
    spot = [jax.random.randint(jax.random.fold_in(own_key, axis), (), 0, shape[axis]) for axis in range(len(shape))]
    entries = entries.at[tuple(spot)].set(least)
    longest = shape.index(max(shape))
    spot[longest] = (spot[longest] + 1) % shape[longest]
    return entries.at[tuple(spot)].set(top_value)


def level_of(stream_key, extent, pieces, least, high):
    level, own = 1.0, jax.random.fold_in(stream_key, 6)
    for axis_at, blocks in pieces:
        heights = jnp.exp(jax.random.uniform(jax.random.fold_in(own, axis_at), (blocks,), jnp.float32, least / len(pieces), high / len(pieces)))
        level = level * jnp.repeat(heights, extent[axis_at] // blocks).reshape([-1 if axis == axis_at else 1 for axis in range(len(extent))])
    return level


def bell_draw(rng, extent, scale, most, pieces=(), held_as=jnp.bfloat16):
    drawn = jax.random.normal(rng, extent, jnp.float32) * scale
    if len(pieces) > 0:
        drawn = level_of(rng, extent, pieces, -0.22, 0.18) * drawn
    return jnp.clip(drawn, min=-most, max=most).astype(held_as)


def setup_inputs(seed: int = 0) -> dict:
    arg_keys = jax.random.split(jax.random.key(seed), 5)
    return {
        "grads": bell_draw(arg_keys[0], (ROWS,), 1.0, 6.0, ((0, 32),)),
        "hessians": jnp.clip(jnp.exp(math.log(0.25) - 2.5308688 * jax.random.uniform(arg_keys[1], (ROWS,), jnp.float32) ** level_of(arg_keys[1], (ROWS,), ((0, 32),), -0.2, 0.2)), 0.019897461, 0.25).astype(jnp.bfloat16),
        "nodes": place_ends(jax.random.randint(arg_keys[2], (ROWS,), 0, NODES), jax.random.fold_in(arg_keys[2], 1), 0, NODES - 1).astype(jnp.int32),
        "bins": place_ends(jax.random.randint(arg_keys[3], (FEATURES, ROWS), 0, BINS), jax.random.fold_in(arg_keys[3], 1), 0, BINS - 1).astype(jnp.int32),
    }


reg_lambda = 1.0


def split_gain(hist):
    left_g = jnp.cumsum(hist[0], axis=-1)
    left_h = jnp.cumsum(hist[1], axis=-1)
    total_g = left_g[..., -1:]
    total_h = left_h[..., -1:]
    gain = left_g * left_g / (left_h + reg_lambda)
    gain = gain + (total_g - left_g) ** 2 / (total_h - left_h + reg_lambda)
    gain = gain - total_g * total_g / (total_h + reg_lambda)
    return jnp.max(gain, axis=(1, 2))


def reference(grads, hessians, nodes, bins):
    grad_f = grads.astype(jnp.float32)
    hess_f = hessians.astype(jnp.float32)
    feat_ids = lax.broadcasted_iota(jnp.int32, (FEAT_DEV, ROWS), 0)
    segments = NODES * FEAT_DEV * BINS

    def one_block(block):
        index = (nodes.astype(jnp.int32)[None, :] * FEAT_DEV + feat_ids) * BINS + block.astype(jnp.int32)
        index = index.reshape(-1)
        sum_g = jax.ops.segment_sum(jnp.broadcast_to(grad_f[None, :], (FEAT_DEV, ROWS)).reshape(-1), index, segments)
        sum_h = jax.ops.segment_sum(jnp.broadcast_to(hess_f[None, :], (FEAT_DEV, ROWS)).reshape(-1), index, segments)
        return jnp.stack([sum_g, sum_h]).reshape(2, NODES, FEAT_DEV, BINS)

    parts = lax.map(one_block, bins.reshape(FEATURES // FEAT_DEV, FEAT_DEV, ROWS))
    histogram = jnp.transpose(parts, (1, 2, 0, 3, 4)).reshape(2, NODES, FEATURES, BINS)
    return histogram, split_gain(histogram)
```

```python
import functools

import jax
import jax.numpy as jnp
from jax import lax
from jax.experimental import pallas as pl
from jax.experimental.pallas import tpu as pltpu
from jax.sharding import PartitionSpec as P

BINS = 256
NODES = 16
LO = 128
HI = BINS // LO
PANEL = 2 * NODES
CHUNK = 2048

reg_lambda = 1.0


def build_panel(gathered, panel, slot, count):
    g = gathered[slot, 0:1, :].astype(jnp.float32)
    h = gathered[slot, 1:2, :].astype(jnp.float32)
    n = gathered[slot, 2:3, :].astype(jnp.float32)
    row = lax.broadcasted_iota(jnp.int32, (PANEL, count), 0)
    value = jnp.where(row % 2 == 0, jnp.broadcast_to(g, row.shape), jnp.broadcast_to(h, row.shape))
    hit = jnp.broadcast_to(n, row.shape) == (row // 2).astype(jnp.float32)
    begin = pl.multiple_of(slot * count, count)
    panel[:, pl.ds(begin, count)] = jnp.where(hit, value, 0.0).astype(jnp.bfloat16)


def one_feature(bins_v, panel, acc, f, feats, chunk):
    rows = bins_v.shape[1]
    total = jnp.zeros((HI * PANEL, LO), jnp.float32)
    base = lax.broadcasted_iota(jnp.int32, (LO // 16, 16, 128), 0) * 16
    ids = (base + lax.broadcasted_iota(jnp.int32, base.shape, 1)).astype(jnp.float32).astype(jnp.bfloat16)
    ids = jnp.concatenate([ids] * (chunk // 128), axis=2)
    for begin in range(0, rows, chunk):
        x = bins_v[pl.ds(f, 1), begin : begin + chunk]
        x = jnp.broadcast_to(x, (16, chunk)).astype(jnp.float32).astype(jnp.bfloat16)
        high = x >= jnp.bfloat16(LO)
        low = jnp.where(high, x - jnp.bfloat16(LO), x)
        part = panel[:, begin : begin + chunk].reshape(PANEL // 16, 16, chunk)
        zero = jnp.zeros_like(part)
        high3 = jnp.broadcast_to(high[None], part.shape)
        left = jnp.concatenate([jnp.where(high3, zero, part), jnp.where(high3, part, zero)], axis=0)
        left = left.reshape(HI * PANEL, chunk)
        hot = jnp.broadcast_to(low[None], ids.shape) == ids
        hot = jnp.where(hot, jnp.ones(ids.shape, jnp.bfloat16), jnp.zeros(ids.shape, jnp.bfloat16))
        hot = hot.reshape(LO, chunk)
        total = total + lax.dot_general(
            left, hot, (((1,), (1,)), ((), ())), preferred_element_type=jnp.float32
        )
    for hi in range(HI):
        acc[hi, pl.ds(f, PANEL, stride=feats), :] = total[hi * PANEL : (hi + 1) * PANEL]


def kernel(
    n_feat, n_rows, pack, bins, hist, best,
    bins_v, gathered, panel, acc, inbox, mine_max, max_in,
    bins_sem, own_sem, ag_send, ag_recv, ex_send, ex_recv, mx_send, mx_recv,
):
    me = lax.axis_index("feat")
    my_row = lax.axis_index("rows")
    feats = bins_v.shape[0]
    count = pack.shape[1]
    share = NODES // n_rows
    span = share * 2 * feats

    load = pltpu.make_async_copy(bins, bins_v, bins_sem)
    load.start()

    barrier = pltpu.get_barrier_semaphore()
    for step in range(1, n_feat):
        pl.semaphore_signal(barrier, inc=1, device_id={"feat": lax.rem(me + step, n_feat)})
    for step in range(1, n_rows):
        pl.semaphore_signal(barrier, inc=1, device_id={"rows": lax.rem(my_row + step, n_rows)})
    pl.semaphore_wait(barrier, n_feat + n_rows - 2)

    def ag_copy(step):
        return pltpu.make_async_remote_copy(
            src_ref=pack,
            dst_ref=gathered.at[me],
            send_sem=ag_send.at[step],
            recv_sem=ag_recv.at[step],
            device_id={"feat": lax.rem(me + step, n_feat)},
        )

    for step in range(1, n_feat):
        ag_copy(step).start()
    own = pltpu.make_async_copy(pack, gathered.at[me], own_sem)
    own.start()
    own.wait()
    for step in range(1, n_feat):
        ag_copy(step).wait()
    load.wait()

    @pl.loop(0, n_feat)
    def _(slot):
        build_panel(gathered, panel, slot, count)

    @pl.loop(0, feats)
    def _(f):
        one_feature(bins_v, panel, acc, f, feats, min(CHUNK, bins_v.shape[1]))

    def ex_copy(step):
        target = lax.rem(my_row + step, n_rows)
        return pltpu.make_async_remote_copy(
            src_ref=acc.at[:, pl.ds(pl.multiple_of(target * span, span), span), :],
            dst_ref=inbox.at[step - 1],
            send_sem=ex_send.at[step],
            recv_sem=ex_recv.at[step],
            device_id={"rows": target},
        )

    for step in range(1, n_rows):
        ex_copy(step).start()
    for step in range(1, n_rows):
        ex_copy(step).wait()

    begin = pl.multiple_of(my_row * span, span)
    tri_in = lax.broadcasted_iota(jnp.int32, (LO, LO), 0)
    tri_out = lax.broadcasted_iota(jnp.int32, (LO, LO), 1)
    tri = (tri_in <= tri_out).astype(jnp.float32)
    lefts = []
    base = None
    for hi in range(HI):
        mine = acc[hi, pl.ds(begin, span), :]
        for step in range(1, n_rows):
            mine = mine + inbox[step - 1, hi]
        for n in range(share):
            for c in range(2):
                at = (n * 2 + c) * feats
                hist[c, n, :, hi * LO : (hi + 1) * LO] = mine[at : at + feats]
        left = lax.dot_general(
            mine, tri, (((1,), (0,)), ((), ())),
            precision=lax.Precision.HIGHEST, preferred_element_type=jnp.float32,
        )
        if base is not None:
            left = left + base
        base = left[:, LO - 1 : LO]
        lefts.append(left.reshape(share, 2, feats, LO))
    whole = base.reshape(share, 2, feats, 1)
    total_g, total_h = whole[:, 0], whole[:, 1]
    top = None
    for left in lefts:
        left_g, left_h = left[:, 0], left[:, 1]
        gain = left_g * left_g / (left_h + reg_lambda)
        gain = gain + (total_g - left_g) ** 2 / (total_h - left_h + reg_lambda)
        gain = gain - total_g * total_g / (total_h + reg_lambda)
        gain = jnp.max(gain, axis=1)
        top = gain if top is None else jnp.maximum(top, gain)
    mine_max[...] = top

    def mx_copy(step):
        return pltpu.make_async_remote_copy(
            src_ref=mine_max,
            dst_ref=max_in.at[step - 1],
            send_sem=mx_send.at[step],
            recv_sem=mx_recv.at[step],
            device_id={"feat": lax.rem(me + step, n_feat)},
        )

    for step in range(1, n_feat):
        mx_copy(step).start()
    for step in range(1, n_feat):
        mx_copy(step).wait()
    for step in range(1, n_feat):
        top = jnp.maximum(top, max_in[step - 1])
    best[...] = jnp.broadcast_to(jnp.max(top, axis=1, keepdims=True), best.shape)


def local(n_feat, n_rows, grads, hessians, nodes, bins):
    feats, rows = bins.shape
    count = grads.shape[0]
    share = NODES // n_rows
    span = share * 2 * feats
    pack = jnp.stack([grads, hessians, nodes.astype(jnp.bfloat16), jnp.zeros_like(grads)])
    vmem = pl.BlockSpec(memory_space=pltpu.VMEM)
    hist, best = pl.pallas_call(
        functools.partial(kernel, n_feat, n_rows),
        out_shape=(
            jax.ShapeDtypeStruct((2, share, feats, BINS), jnp.float32),
            jax.ShapeDtypeStruct((share, 128), jnp.float32),
        ),
        in_specs=[vmem, pl.BlockSpec(memory_space=pl.ANY)],
        out_specs=(vmem, vmem),
        scratch_shapes=[
            pltpu.VMEM((feats, rows), jnp.int32),
            pltpu.VMEM((n_feat, 4, count), jnp.bfloat16),
            pltpu.VMEM((PANEL, rows), jnp.bfloat16),
            pltpu.VMEM((HI, PANEL * feats, LO), jnp.float32),
            pltpu.VMEM((max(n_rows - 1, 1), HI, span, LO), jnp.float32),
            pltpu.VMEM((share, LO), jnp.float32),
            pltpu.VMEM((max(n_feat - 1, 1), share, LO), jnp.float32),
            pltpu.SemaphoreType.DMA,
            pltpu.SemaphoreType.DMA,
            pltpu.SemaphoreType.DMA((n_feat,)),
            pltpu.SemaphoreType.DMA((n_feat,)),
            pltpu.SemaphoreType.DMA((n_rows,)),
            pltpu.SemaphoreType.DMA((n_rows,)),
            pltpu.SemaphoreType.DMA((n_feat,)),
            pltpu.SemaphoreType.DMA((n_feat,)),
        ],
        compiler_params=pltpu.CompilerParams(
            collective_id=0, has_side_effects=True, vmem_limit_bytes=56 << 20
        ),
        name="tree_level",
    )(pack, bins)
    return hist, best[:, 0]


def solution(mesh):
    return jax.shard_map(
        functools.partial(local, mesh.shape["feat"], mesh.shape["rows"]),
        mesh=mesh,
        in_specs=(P(("rows", "feat")), P(("rows", "feat")), P(("rows", "feat")), P("feat", "rows")),
        out_specs=(P(None, "rows", "feat", None), P("rows")),
        check_vma=False,
    )
```

```python
import functools

import jax
import jax.numpy as jnp
from jax import lax
from jax.experimental import pallas as pl
from jax.experimental.pallas import tpu as pltpu
from jax.sharding import PartitionSpec as P

BINS = 256
NODES = 16
LO = 128
HI = BINS // LO
PANEL = 2 * NODES
CHUNK = 1024
UNROLL = 4

reg_lambda = 1.0


def build_panel(gathered, panel, slot, count):
    g = gathered[slot, 0:1, :].astype(jnp.float32)
    h = gathered[slot, 1:2, :].astype(jnp.float32)
    n = gathered[slot, 2:3, :].astype(jnp.float32)
    row = lax.broadcasted_iota(jnp.int32, (PANEL, count), 0)
    value = jnp.where(row % 2 == 0, jnp.broadcast_to(g, row.shape), jnp.broadcast_to(h, row.shape))
    hit = jnp.broadcast_to(n, row.shape) == (row // 2).astype(jnp.float32)
    begin = pl.multiple_of(slot * count, count)
    panel[:, pl.ds(begin, count)] = jnp.where(hit, value, 0.0).astype(jnp.bfloat16)


def one_feature(bins_v, panel, acc, f, feats, chunk):
    rows = bins_v.shape[1]
    total = jnp.zeros((LO, HI * PANEL), jnp.float32)
    base = lax.broadcasted_iota(jnp.int32, (LO // 16, 16, 128), 0) * 16
    ids = (base + lax.broadcasted_iota(jnp.int32, base.shape, 1)).astype(jnp.float32).astype(jnp.bfloat16)
    ids = jnp.concatenate([ids] * (chunk // 128), axis=2)
    for begin in range(0, rows, chunk):
        x = bins_v[pl.ds(f, 1), begin : begin + chunk]
        x = jnp.broadcast_to(x, (16, chunk)).astype(jnp.float32).astype(jnp.bfloat16)
        high = x >= jnp.bfloat16(LO)
        low = jnp.where(high, x - jnp.bfloat16(LO), x)
        part = panel[:, begin : begin + chunk].reshape(PANEL // 16, 16, chunk)
        zero = jnp.zeros_like(part)
        high3 = jnp.broadcast_to(high[None], part.shape)
        left = jnp.concatenate([jnp.where(high3, zero, part), jnp.where(high3, part, zero)], axis=0)
        left = left.reshape(HI * PANEL, chunk)
        hot = jnp.broadcast_to(low[None], ids.shape) == ids
        hot = jnp.where(hot, jnp.ones(ids.shape, jnp.bfloat16), jnp.zeros(ids.shape, jnp.bfloat16))
        hot = hot.reshape(LO, chunk)
        total = total + lax.dot_general(
            hot, left, (((1,), (1,)), ((), ())), preferred_element_type=jnp.float32
        )
    total = total.T
    for hi in range(HI):
        acc[hi, pl.ds(f, PANEL, stride=feats), :] = total[hi * PANEL : (hi + 1) * PANEL]


def kernel(
    n_feat, n_rows, pack, bins, hist, best,
    bins_v, gathered, panel, acc, inbox, mine_max, max_in,
    bins_sem, own_sem, ag_send, ag_recv, ex_send, ex_recv, mx_send, mx_recv,
):
    me = lax.axis_index("feat")
    my_row = lax.axis_index("rows")
    feats = bins_v.shape[0]
    count = pack.shape[1]
    share = NODES // n_rows
    span = share * 2 * feats

    load = pltpu.make_async_copy(bins, bins_v, bins_sem)
    load.start()

    barrier = pltpu.get_barrier_semaphore()
    for step in range(1, n_feat):
        pl.semaphore_signal(barrier, inc=1, device_id={"feat": lax.rem(me + step, n_feat)})
    for step in range(1, n_rows):
        pl.semaphore_signal(barrier, inc=1, device_id={"rows": lax.rem(my_row + step, n_rows)})
    pl.semaphore_wait(barrier, n_feat + n_rows - 2)

    def ag_copy(step):
        return pltpu.make_async_remote_copy(
            src_ref=pack,
            dst_ref=gathered.at[me],
            send_sem=ag_send.at[step],
            recv_sem=ag_recv.at[step],
            device_id={"feat": lax.rem(me + step, n_feat)},
        )

    for step in range(1, n_feat):
        ag_copy(step).start()
    own = pltpu.make_async_copy(pack, gathered.at[me], own_sem)
    own.start()
    own.wait()
    for step in range(1, n_feat):
        ag_copy(step).wait()
    load.wait()

    @pl.loop(0, n_feat)
    def _(slot):
        build_panel(gathered, panel, slot, count)

    @pl.loop(0, feats // UNROLL)
    def _(group):
        for at in range(UNROLL):
            one_feature(bins_v, panel, acc, group * UNROLL + at, feats, min(CHUNK, bins_v.shape[1]))

    def ex_copy(step):
        target = lax.rem(my_row + step, n_rows)
        return pltpu.make_async_remote_copy(
            src_ref=acc.at[:, pl.ds(pl.multiple_of(target * span, span), span), :],
            dst_ref=inbox.at[step - 1],
            send_sem=ex_send.at[step],
            recv_sem=ex_recv.at[step],
            device_id={"rows": target},
        )

    for step in range(1, n_rows):
        ex_copy(step).start()
    for step in range(1, n_rows):
        ex_copy(step).wait()

    begin = pl.multiple_of(my_row * span, span)
    tri_in = lax.broadcasted_iota(jnp.int32, (LO, LO), 0)
    tri_out = lax.broadcasted_iota(jnp.int32, (LO, LO), 1)
    tri = (tri_in <= tri_out).astype(jnp.float32)
    lefts = []
    base = None
    for hi in range(HI):
        mine = acc[hi, pl.ds(begin, span), :]
        for step in range(1, n_rows):
            mine = mine + inbox[step - 1, hi]
        for n in range(share):
            for c in range(2):
                at = (n * 2 + c) * feats
                hist[c, n, :, hi * LO : (hi + 1) * LO] = mine[at : at + feats]
        left = lax.dot_general(
            mine, tri, (((1,), (0,)), ((), ())),
            precision=lax.Precision.HIGHEST, preferred_element_type=jnp.float32,
        )
        if base is not None:
            left = left + base
        base = left[:, LO - 1 : LO]
        lefts.append(left.reshape(share, 2, feats, LO))
    whole = base.reshape(share, 2, feats, 1)
    total_g, total_h = whole[:, 0], whole[:, 1]
    top = None
    for left in lefts:
        left_g, left_h = left[:, 0], left[:, 1]
        gain = left_g * left_g / (left_h + reg_lambda)
        gain = gain + (total_g - left_g) ** 2 / (total_h - left_h + reg_lambda)
        gain = gain - total_g * total_g / (total_h + reg_lambda)
        gain = jnp.max(gain, axis=1)
        top = gain if top is None else jnp.maximum(top, gain)
    mine_max[...] = top

    def mx_copy(step):
        return pltpu.make_async_remote_copy(
            src_ref=mine_max,
            dst_ref=max_in.at[step - 1],
            send_sem=mx_send.at[step],
            recv_sem=mx_recv.at[step],
            device_id={"feat": lax.rem(me + step, n_feat)},
        )

    for step in range(1, n_feat):
        mx_copy(step).start()
    for step in range(1, n_feat):
        mx_copy(step).wait()
    for step in range(1, n_feat):
        top = jnp.maximum(top, max_in[step - 1])
    best[...] = jnp.broadcast_to(jnp.max(top, axis=1, keepdims=True), best.shape)


def local(n_feat, n_rows, grads, hessians, nodes, bins):
    feats, rows = bins.shape
    count = grads.shape[0]
    share = NODES // n_rows
    span = share * 2 * feats
    pack = jnp.stack([grads, hessians, nodes.astype(jnp.bfloat16), jnp.zeros_like(grads)])
    vmem = pl.BlockSpec(memory_space=pltpu.VMEM)
    hist, best = pl.pallas_call(
        functools.partial(kernel, n_feat, n_rows),
        out_shape=(
            jax.ShapeDtypeStruct((2, share, feats, BINS), jnp.float32),
            jax.ShapeDtypeStruct((share, 128), jnp.float32),
        ),
        in_specs=[vmem, pl.BlockSpec(memory_space=pl.ANY)],
        out_specs=(vmem, vmem),
        scratch_shapes=[
            pltpu.VMEM((feats, rows), jnp.int32),
            pltpu.VMEM((n_feat, 4, count), jnp.bfloat16),
            pltpu.VMEM((PANEL, rows), jnp.bfloat16),
            pltpu.VMEM((HI, PANEL * feats, LO), jnp.float32),
            pltpu.VMEM((max(n_rows - 1, 1), HI, span, LO), jnp.float32),
            pltpu.VMEM((share, LO), jnp.float32),
            pltpu.VMEM((max(n_feat - 1, 1), share, LO), jnp.float32),
            pltpu.SemaphoreType.DMA,
            pltpu.SemaphoreType.DMA,
            pltpu.SemaphoreType.DMA((n_feat,)),
            pltpu.SemaphoreType.DMA((n_feat,)),
            pltpu.SemaphoreType.DMA((n_rows,)),
            pltpu.SemaphoreType.DMA((n_rows,)),
            pltpu.SemaphoreType.DMA((n_feat,)),
            pltpu.SemaphoreType.DMA((n_feat,)),
        ],
        compiler_params=pltpu.CompilerParams(
            collective_id=0, has_side_effects=True, vmem_limit_bytes=56 << 20
        ),
        name="tree_level",
    )(pack, bins)
    return hist, best[:, 0]


def solution(mesh):
    return jax.shard_map(
        functools.partial(local, mesh.shape["feat"], mesh.shape["rows"]),
        mesh=mesh,
        in_specs=(P(("rows", "feat")), P(("rows", "feat")), P(("rows", "feat")), P("feat", "rows")),
        out_specs=(P(None, "rows", "feat", None), P("rows")),
        check_vma=False,
    )
```
